32 devices in a mesh: groups: 2 (over y), ctx: 8 (over z, x), head: 2 (over core).
Axes of the slice: x: 2, y: 2, z: 4, core: 2. Of those that a mesh axis runs over, the one named last changes fastest.
Arguments:
- queries: bfloat16 [2048, 2048], P(('groups', 'ctx'), 'head'), parts along dimension 0, may hold values from -16 to 16
- key_states: bfloat16 [2048, 1024], P(('groups', 'ctx'), 'head'), parts along dimension 0, may hold values from -16 to 16
- value_states: bfloat16 [2048, 1024], P(('groups', 'ctx'), 'head'), parts along dimension 0, may hold values from -6 to 6
- out_grad: bfloat16 [2048, 2048], P(('groups', 'ctx'), 'head'), parts along dimension 0, may hold values from -6 to 6
- doc_ids: int32 [32], P('groups'), parts along dimension 0, may hold values from 0 to 5, never falling along the last dimension, each value on 1 to 8 neighbouring positions
- int_pos: int32 [128], P('groups'), parts along dimension 0, may hold values from 0 to 127, as said below
- hidden: bfloat16 [128, 4608], P('groups', 'ctx'), parts along dimension 0, may hold values from -6 to 6
- upstream: bfloat16 [128, 4608], P('groups', 'ctx'), parts along dimension 0, may hold values from -3 to 3
- w_query: bfloat16 [4608, 2048], P('ctx', 'head'), may hold values from -0.09375 to 0.09375
- w_key: bfloat16 [4608, 1024], P('ctx', 'head'), may hold values from -0.09375 to 0.09375
- w_value: bfloat16 [4608, 1024], P('ctx', 'head'), may hold values from -0.09375 to 0.09375
- rotation: float32 [8, 4608], P(None, 'ctx'), may hold values from -0.09375 to 0.09375
- projection: float32 [8, 4608], P(None, 'ctx'), may hold values from -0.09375 to 0.09375
- rank_bias: float32 [8], replicated, may hold values from -4 to 4
Outputs:
- grad_rot: float32 [16, 4608], P('groups', 'ctx'), parts along dimension 0
- grad_proj: float32 [16, 4608], P('groups', 'ctx'), parts along dimension 0
- grad_bias: float32 [16], P('groups'), parts along dimension 0
The draws below stay inside these ranges and needn't reach their ends.
There are 2 independent parts, one for each index of `groups`. The reference program is written for one: setup_inputs(seed, part) draws one part's arguments, and reference() takes and returns one part's arrays. A program takes and returns all parts, laid end to end along the dimension named above; an argument that names none is the same for every part. Nothing has to cross between parts.
Inputs may be any that keep to these rules, and one draw needn't show every extreme that they name: `doc_ids`: ids never fall along the blocks; each document covers 1 to 8 consecutive blocks, and one covers exactly 8. `int_pos`: each aligned group of 8 entries belongs to one block of 128 tokens and holds distinct token indices inside that block in rising order.
All inputs are finite; a program needn't handle non-finite values.
Results may differ from the reference program's by a relative error of at most 0.004.
The reference program's roundings to bfloat16 on the way count: a program that leaves them out, or rounds other values in their place, can miss the bound.
Values may be sent and summed in bfloat16 or wider, within the bound.
A program may use at most 64 MiB of HBM per device.

```python
import math
import jax
import jax.numpy as jnp
import numpy as np
from jax import lax

D = 4608
QH = 16
KVH = 8
HD = 128
RANK = 8
BLK = 64
POS_DEV = 8
DOCS = 6
TOK_DEV = 128
CTXLEN = 1024
NBLK = 16
DOC_MOST = 8
POS_ALL = 64


def draw_int_pos(key, part):
    block_count = POS_ALL // POS_DEV
    block_keys = jax.random.split(jax.random.fold_in(key, 11), block_count)

    def draw_block(block_key):
        shuffled = jax.random.permutation(block_key, TOK_DEV)
        return jnp.sort(shuffled[:POS_DEV]).astype(jnp.int32)
    return jax.vmap(draw_block)(block_keys).reshape(POS_ALL)


def scaled_rows(key, head_count, salt):
    salted = jax.random.fold_in(key, salt)
    base_key, scale_key = jax.random.split(salted)
    base_vals = jax.random.truncated_normal(base_key, -4.0, 4.0, (CTXLEN, head_count, HD), jnp.float32)
    top_scale = 4.0
    row_scale = jnp.exp(jax.random.uniform(scale_key, (CTXLEN, head_count, 1), jnp.float32, 0.0, math.log(top_scale)))
    return (base_vals * row_scale).reshape(CTXLEN, head_count * HD).astype(jnp.bfloat16)


def draw_queries(key, part):
    return scaled_rows(key, QH, 21)


def draw_key_states(key, part):
    return scaled_rows(key, KVH, 22)


def block_scale(stream_key, extent, shards, smallest, high):
    factor_of = 1.0
    for position, parts in shards:
        draws = jax.random.uniform(jax.random.fold_in(jax.random.fold_in(stream_key, 6), position), (parts,), jnp.float32, smallest / len(shards), high / len(shards))
        factor_of = factor_of * jnp.repeat(jnp.exp(draws), extent[position] // parts).reshape((-1,) + (1,) * (len(extent) - 1 - position))
    return factor_of


def split_up(number_of, total, most, slope):
    loads = [(1 << 20) // math.isqrt(rank ** slope) + 1 for rank in range(2, number_of + 1)]
    surplus, counts = total - most - (number_of - 1), [1] * (number_of - 1)
    while surplus > 0:
        free = [i for i in range(number_of - 1) if counts[i] < most]
        pool, budget = sum([loads[i] for i in free]), surplus
        for i in free:
            extra = min(most - counts[i], max(1, budget * loads[i] // pool), surplus)
            counts[i] = counts[i] + extra
            surplus = surplus - extra
    return np.array([most] + counts)


def ragged(stream_key, count, total, bound, slope):
    if count == 2:
        one = jax.random.randint(stream_key, (), max(1, total - bound), min(bound, total - 1) + 1)
        return jnp.stack([one, total - one])
    lengths = jnp.asarray(split_up(count, total, bound, slope), jnp.int32)
    couples = (count - 1) // 2
    source_of, receiver = lengths[1:1 + 2 * couples:2], lengths[2:2 + 2 * couples:2]
    margin = jnp.minimum(source_of - 1, bound - receiver)
    passed = jax.random.randint(jax.random.fold_in(stream_key, 1), (couples,), 0, 1 << 20) % (margin + 1)
    lengths = lengths.at[1:1 + 2 * couples:2].set(source_of - passed).at[2:2 + 2 * couples:2].set(receiver + passed)
    return lengths[jax.random.permutation(jax.random.fold_in(stream_key, 2), count)]


def centred(rng, extent, width, bound, shards=(), kind=jnp.bfloat16):
    level = block_scale(rng, extent, shards, -0.22, 0.18) if shards else 1.0
    values = jax.random.normal(rng, extent, jnp.float32) * width * level
    return jnp.minimum(jnp.maximum(values, -bound), bound).astype(kind)


def setup_inputs(seed: int = 0, part: int = 0) -> dict:
    key_of = jax.random.split(jax.random.key(seed), 15)
    own_keys = jax.random.split(jax.random.fold_in(key_of[14], part), 15)
    queries = draw_queries(jax.random.fold_in(jax.random.fold_in(key_of[14], part), 71), part)
    key_states = draw_key_states(jax.random.fold_in(jax.random.fold_in(key_of[14], part), 71), part)
    value_states = centred(own_keys[2], (CTXLEN, KVH * HD), 1.0, 6.0, ((0, 8), (1, 2)))
    out_grad = centred(own_keys[3], (CTXLEN, QH * HD), 1.0, 6.0, ((0, 8), (1, 2)))
    doc_ids = jnp.searchsorted(jnp.cumsum(ragged(own_keys[4], DOCS, NBLK, DOC_MOST, 2)), jnp.arange(NBLK), side="right").astype(jnp.int32)
    int_pos = draw_int_pos(jax.random.fold_in(jax.random.fold_in(key_of[14], part), 71), part)
    hidden = centred(own_keys[6], (POS_ALL, D), 1.0, 6.0, ((1, 8),))
    upstream = centred(own_keys[7], (POS_ALL, D), 0.2, 3.0, ((1, 8),))
    w_query = centred(key_of[8], (D, QH * HD), D ** -0.5, 0.09375, ((0, 8), (1, 2)))
    w_key = centred(key_of[9], (D, KVH * HD), D ** -0.5, 0.09375, ((0, 8), (1, 2)))
    w_value = centred(key_of[10], (D, KVH * HD), D ** -0.5, 0.09375, ((0, 8), (1, 2)))
    rotation = centred(key_of[11], (RANK, D), D ** -0.5, 0.09375, ((1, 8),), jnp.float32)
    projection = centred(key_of[12], (RANK, D), D ** -0.5, 0.09375, ((1, 8),), jnp.float32)
    rank_bias = centred(key_of[13], (RANK,), 1.0, 4.0, (), jnp.float32)
    return dict(queries=queries, key_states=key_states, value_states=value_states, out_grad=out_grad, doc_ids=doc_ids, int_pos=int_pos, hidden=hidden, upstream=upstream, w_query=w_query, w_key=w_key, w_value=w_value, rotation=rotation, projection=projection, rank_bias=rank_bias)


scale_q = 1.0 / 12.0
soft_cap = 50.0

def capping(dot_vals):
    return soft_cap * jnp.tanh(dot_vals * scale_q / soft_cap)

def reference(queries, key_states, value_states, out_grad, doc_ids, int_pos, hidden, upstream, w_query, w_key, w_value, rotation, projection, rank_bias):
    length = queries.shape[0]
    per_group = QH // KVH
    query_all = queries.reshape(length, QH, HD)
    key_all = key_states.reshape(length, KVH, HD)
    value_all = value_states.reshape(length, KVH, HD)
    grad_all = out_grad.reshape(length, QH, HD)
    tok_pos = jnp.arange(length, dtype=jnp.int32)
    tok_doc = doc_ids[tok_pos // BLK]
    pick_pos = jnp.arange(POS_ALL, dtype=jnp.int32) // POS_DEV * TOK_DEV + int_pos
    pick_doc = tok_doc[pick_pos]
    q_block = math.gcd(length, 512)
    block_count = length // q_block

    def forward_head(head_no):
        query_h = query_all[:, head_no]
        key_h = key_all[:, head_no // per_group]
        value_h = value_all[:, head_no // per_group]

        def forward_block(block_no):
            query_rows = lax.dynamic_slice_in_dim(query_h, block_no * q_block, q_block, 0)
            rows_pos = lax.dynamic_slice_in_dim(tok_pos, block_no * q_block, q_block, 0)
            rows_doc = lax.dynamic_slice_in_dim(tok_doc, block_no * q_block, q_block, 0)
            capped = capping(jnp.dot(query_rows, key_h.T, preferred_element_type=jnp.float32))
            visible = (tok_pos[None, :] <= rows_pos[:, None]) & (tok_doc[None, :] == rows_doc[:, None])
            weights = jnp.where(visible, jnp.exp(capped), 0.0)
            return (lax.optimization_barrier(jnp.sum(weights, axis=1)), jnp.dot(weights.astype(jnp.bfloat16), value_h, preferred_element_type=jnp.float32))
        z_blocks, numer_blocks = lax.map(forward_block, jnp.arange(block_count, dtype=jnp.int32))
        return (z_blocks.reshape(length), numer_blocks.reshape(length, HD))
    z_all, numer_all = lax.map(forward_head, jnp.arange(QH, dtype=jnp.int32))
    outputs = numer_all / z_all[..., None]
    row_delta = lax.optimization_barrier(jnp.sum(jnp.transpose(grad_all, (1, 0, 2)).astype(jnp.float32) * outputs, axis=-1))

    def query_grad(head_no):
        query_h = query_all[:, head_no]
        grad_h = grad_all[:, head_no]
        key_h = key_all[:, head_no // per_group]
        value_h = value_all[:, head_no // per_group]
        pick_query = query_h[pick_pos]
        pick_grad = grad_h[pick_pos]
        capped = capping(jnp.dot(pick_query, key_h.T, preferred_element_type=jnp.float32))
        visible = (tok_pos[None, :] <= pick_pos[:, None]) & (tok_doc[None, :] == pick_doc[:, None])
        weights = jnp.where(visible, jnp.exp(capped), 0.0) * (1.0 - (capped / soft_cap) ** 2)
        prob_grad = jnp.dot(pick_grad, value_h.T, preferred_element_type=jnp.float32)
        main_sum = jnp.dot((weights * prob_grad).astype(jnp.bfloat16), key_h, preferred_element_type=jnp.float32)
        side_sum = jnp.dot(weights.astype(jnp.bfloat16), key_h, preferred_element_type=jnp.float32)
        z_pick = z_all[head_no][pick_pos]
        delta_pick = row_delta[head_no][pick_pos]
        return scale_q * (main_sum - delta_pick[:, None] * side_sum) / z_pick[:, None]
    dq_heads = lax.map(query_grad, jnp.arange(QH, dtype=jnp.int32))
    dq_rows = jnp.transpose(dq_heads, (1, 0, 2)).reshape(POS_ALL, QH * HD).astype(jnp.bfloat16)

    def key_grad(head_no):
        query_h = query_all[:, head_no]
        grad_h = grad_all[:, head_no]
        key_pick = key_all[:, head_no // per_group][pick_pos]
        value_pick = value_all[:, head_no // per_group][pick_pos]
        capped = capping(jnp.dot(query_h, key_pick.T, preferred_element_type=jnp.float32))
        visible = (pick_pos[None, :] <= tok_pos[:, None]) & (pick_doc[None, :] == tok_doc[:, None])
        probs = jnp.where(visible, jnp.exp(capped), 0.0) / z_all[head_no][:, None]
        prob_grad = jnp.dot(grad_h, value_pick.T, preferred_element_type=jnp.float32)
        dscore = probs * (prob_grad - row_delta[head_no][:, None]) * (1.0 - (capped / soft_cap) ** 2)
        value_g = jnp.dot(probs.astype(jnp.bfloat16).T, grad_h, preferred_element_type=jnp.float32)
        key_g = scale_q * jnp.dot(dscore.astype(jnp.bfloat16).T, query_h, preferred_element_type=jnp.float32)
        return (key_g, value_g)
    key_heads_g, value_heads_g = lax.map(key_grad, jnp.arange(QH, dtype=jnp.int32))
    key_sum = key_heads_g.reshape(KVH, per_group, POS_ALL, HD).sum(axis=1)
    value_sum = value_heads_g.reshape(KVH, per_group, POS_ALL, HD).sum(axis=1)
    dk_rows = jnp.transpose(key_sum, (1, 0, 2)).reshape(POS_ALL, KVH * HD).astype(jnp.bfloat16)
    dv_rows = jnp.transpose(value_sum, (1, 0, 2)).reshape(POS_ALL, KVH * HD).astype(jnp.bfloat16)
    resid_grad = jnp.dot(dq_rows, w_query.T, preferred_element_type=jnp.float32)
    resid_grad = resid_grad + jnp.dot(dk_rows, w_key.T, preferred_element_type=jnp.float32)
    resid_grad = resid_grad + jnp.dot(dv_rows, w_value.T, preferred_element_type=jnp.float32)
    resid_grad = resid_grad + upstream.astype(jnp.float32)
    hidden_wide = hidden.astype(jnp.float32)
    rank_grad = jnp.dot(resid_grad, rotation.T, precision=lax.Precision.HIGHEST)
    rank_state = jnp.dot(hidden_wide, (projection - rotation).T, precision=lax.Precision.HIGHEST) + rank_bias[None, :]
    grad_bias = lax.optimization_barrier(jnp.sum(rank_grad, axis=0))
    grad_proj = jnp.dot(rank_grad.T, hidden_wide, precision=lax.Precision.HIGHEST)
    grad_rot = jnp.dot(rank_state.T, resid_grad, precision=lax.Precision.HIGHEST) - grad_proj
    return (grad_rot, grad_proj, grad_bias)
```

```python
import functools

import jax
import jax.numpy as jnp
from jax import lax
from jax.experimental import pallas as pl
from jax.experimental.pallas import tpu as pltpu
from jax.sharding import PartitionSpec as P

HD = 128
BLK = 64
POS_DEV = 8
LANES = 128

scale_q = 1.0 / 12.0
soft_cap = 50.0

MESH = pl.DeviceIdType.MESH
HIGHEST = lax.Precision.HIGHEST
F32 = jnp.float32
BF16 = jnp.bfloat16


def round_up(value, multiple):
    return (value + multiple - 1) // multiple * multiple


def dot_nt(left, right, precision=None):
    return lax.dot_general(
        left, right, (((1,), (1,)), ((), ())), preferred_element_type=F32, precision=precision
    )


def dot_tn(left, right):
    return lax.dot_general(left, right, (((0,), (0,)), ((), ())), preferred_element_type=F32)


def kernel(
    n,
    q_ref, k_ref, v_ref, g_ref, doc_ref, pos_ref, hidden_ref, up_ref,
    wq_hbm, wk_hbm, wv_hbm, rot_ref, proj_ref, bias_ref,
    rot_out, proj_out, bias_out,
    kbuf, vbuf, qa, ga, num, zs, ms, kp, vp, part, part_in, dq_rows, kv_rows,
    st_all, rg_all, gr_own, gr_in, wq, wk, wv,
    w_sem, ch_send, ch_recv, ex_send, ex_recv, st_send, st_recv, dq_send, dq_recv,
    pt_send, pt_recv, kv_send, kv_recv, rg_send, rg_recv, gr_send, gr_recv,
):
    me = lax.axis_index("ctx")
    core = lax.axis_index("head")
    odd = lax.rem(me, 2)
    partner = me + 1 - 2 * odd
    after = lax.rem(me + 2, n)
    halo = n // 2
    chain = halo // 2
    tokens = q_ref.shape[0]
    kv_width = k_ref.shape[1]
    heads = kv_width // HD
    positions = n * POS_DEV
    lanes = st_all.shape[2]
    width = hidden_ref.shape[1]
    rows = 2 * tokens + 2 * POS_DEV
    npick = kp.shape[0] * POS_DEV

    barrier = pltpu.get_barrier_semaphore()
    for k in range(1, n):
        for c in range(2):
            pl.semaphore_signal(
                barrier, inc=1, device_id={"ctx": lax.rem(me + k, n), "head": c},
                device_id_type=MESH,
            )
    pl.semaphore_signal(barrier, inc=1, device_id={"head": 1 - core}, device_id_type=MESH)

    loads = [
        pltpu.make_async_copy(src, dst, w_sem.at[i])
        for i, (src, dst) in enumerate(((wq_hbm, wq), (wk_hbm, wk), (wv_hbm, wv)))
    ]
    for load in loads:
        load.start()
    kbuf[0] = k_ref[...]
    vbuf[0] = v_ref[...]

    def send(src, dst, send_sem, recv_sem, **where):
        return pltpu.make_async_remote_copy(
            src_ref=src, dst_ref=dst, send_sem=send_sem, recv_sem=recv_sem,
            device_id=where, device_id_type=MESH,
        )

    bufs = (kbuf, vbuf)

    def chain_copy(j, p):
        return send(
            bufs[p].at[2 * j - 2], bufs[p].at[2 * j], ch_send.at[j - 1, p],
            ch_recv.at[j - 1, p], ctx=after,
        )

    def exchange_copy(j, p, to_slot, m):
        return send(
            bufs[p].at[2 * j], bufs[p].at[to_slot], ex_send.at[m, p], ex_recv.at[m, p],
            ctx=partner,
        )

    def exchange(j, run):
        if j < chain:
            @pl.when(odd == 0)
            def _():
                for p in range(2):
                    run(exchange_copy(j, p, 2 * j + 1, j))
        if j > 0:
            @pl.when(odd == 1)
            def _():
                for p in range(2):
                    run(exchange_copy(j, p, 2 * j - 1, j - 1))

    row8 = lax.broadcasted_iota(jnp.int32, (POS_DEV, LANES), 0)
    lane8 = lax.broadcasted_iota(jnp.int32, (POS_DEV, LANES), 1)

    def slot_pos(k):
        block = lax.rem(me - k + n, n)
        return [pos_ref[block * POS_DEV + r] for r in range(POS_DEV)]

    def column(values):
        out = jnp.zeros((POS_DEV, LANES), jnp.int32)
        for r in range(POS_DEV):
            out = jnp.where(row8 == r, values[r], out)
        return out

    def one_hot(values):
        return jnp.where(column(values) == lane8, 1.0, 0.0).astype(BF16)

    blocks = tokens // BLK
    starts = []
    for b in range(blocks):
        mine = doc_ref[me * blocks + b]
        starts.append(
            lax.fori_loop(
                0, doc_ref.shape[0],
                lambda i, s, mine=mine: s + jnp.where(doc_ref[i] < mine, BLK, 0),
                jnp.int32(0),
            )
        )

    def start_of(position):
        out = jnp.zeros(position.shape, jnp.int32) + starts[0]
        for b in range(1, blocks):
            out = jnp.where(position >= b * BLK, starts[b], out)
        return out

    mine = column(slot_pos(0))
    own = lax.broadcasted_iota(jnp.int32, (tokens, LANES), 0)
    local_pos = jnp.concatenate([own, own, mine, mine], axis=0)
    row_pos = local_pos + me * tokens
    row_start = start_of(local_pos)
    lane_all = lax.broadcasted_iota(jnp.int32, (rows, LANES), 1)

    pick = one_hot(slot_pos(0))
    q_pick = jnp.dot(pick, q_ref[...], preferred_element_type=F32)
    g_pick = jnp.dot(pick, g_ref[...], preferred_element_type=F32)
    for h in range(heads):
        a, b, c = 2 * h * HD, (2 * h + 1) * HD, (2 * h + 2) * HD
        for dst, src, picked in ((qa, q_ref, q_pick), (ga, g_ref, g_pick)):
            dst[h, :tokens] = src[:, a:b]
            dst[h, tokens : 2 * tokens] = src[:, b:c]
            dst[h, 2 * tokens :] = jnp.concatenate(
                [picked[:, a:b], picked[:, b:c]], axis=0
            ).astype(BF16)

    hidden_wide = hidden_ref[...].astype(F32)
    state = dot_nt(proj_ref[...] - rot_ref[...], hidden_wide, HIGHEST)
    if lanes > positions:
        st_all[me] = jnp.zeros(st_all.shape[1:], F32)
    st_all[me, :, :positions] = state

    pl.semaphore_wait(barrier, 2 * n - 1)

    for p in range(2):
        chain_copy(1, p).start()
    exchange(0, lambda copy: copy.start())

    def to_all(src, dst, send_sems, recv_sems):
        def copies():
            return [
                send(
                    src, dst.at[me], send_sems.at[k - 1], recv_sems.at[me],
                    ctx=lax.rem(me + k, n),
                )
                for k in range(1, n)
            ]

        def receives():
            return [
                send(
                    src, dst.at[lax.rem(me - k + n, n)], send_sems.at[k - 1],
                    recv_sems.at[lax.rem(me - k + n, n)], ctx=lax.rem(me + k, n),
                )
                for k in range(1, n)
            ]

        return copies, receives

    st_copies, st_receives = to_all(st_all.at[me], st_all, st_send, st_recv)
    for copy in st_copies():
        copy.start()

    if npick > (halo + 1) * POS_DEV:
        kp[halo + 1 :] = jnp.zeros((kp.shape[0] - halo - 1,) + kp.shape[1:], F32)
        vp[halo + 1 :] = jnp.zeros((vp.shape[0] - halo - 1,) + vp.shape[1:], F32)

    def visit(k):
        base = (me - k) * tokens
        key_pos = lane_all + base
        visible = (key_pos >= row_start) & (key_pos <= row_pos)
        hot = one_hot(slot_pos(k))
        kp[k] = jnp.dot(hot, kbuf[k], preferred_element_type=F32)
        vp[k] = jnp.dot(hot, vbuf[k], preferred_element_type=F32)
        for h in range(heads):
            cols = slice(h * HD, (h + 1) * HD)
            keys = kbuf[k, :, cols]
            values = vbuf[k, :, cols]
            bent = jnp.tanh(dot_nt(qa[h], keys) * (scale_q / soft_cap))
            weights = jnp.where(visible, jnp.exp(soft_cap * bent), 0.0)
            z_new = jnp.broadcast_to(jnp.sum(weights, axis=1, keepdims=True), (rows, LANES))
            num_new = jnp.dot(weights.astype(BF16), values, preferred_element_type=F32)
            bent_pick = bent[2 * tokens :]
            side = weights[2 * tokens :] * (1.0 - bent_pick * bent_pick)
            main = side * dot_nt(ga[h, 2 * tokens :], values)
            both = jnp.concatenate([main, side], axis=0).astype(BF16)
            ms_new = jnp.dot(both, keys, preferred_element_type=F32)
            if k == 0:
                zs[h], num[h], ms[h] = z_new, num_new, ms_new
            else:
                zs[h] += z_new
                num[h] += num_new
                ms[h] += ms_new

    visit(0)
    for j in range(1, chain + 1):
        for p in range(2):
            chain_copy(j, p).wait_recv()
            if j < chain:
                chain_copy(j + 1, p).start()
        exchange(j, lambda copy: copy.start())
        visit(2 * j)
        for p in range(2):
            send(
                bufs[p].at[0], bufs[p].at[2 * j - 1], ex_send.at[j - 1, p],
                ex_recv.at[j - 1, p], ctx=partner,
            ).wait_recv()
        visit(2 * j - 1)

    deltas = []
    for h in range(heads):
        inv = num[h] / zs[h]
        delta = jnp.sum(ga[h].astype(F32) * inv, axis=1, keepdims=True)
        deltas.append(delta)
        d_pick = delta[2 * tokens :]
        main, side = ms[h, : 2 * POS_DEV], ms[h, 2 * POS_DEV :]
        dq = scale_q * (main - d_pick * side) / zs[h, 2 * tokens :]
        for i in range(2):
            at = (2 * h + i) * HD
            dq_rows[me, :, at : at + HD] = dq[i * POS_DEV : (i + 1) * POS_DEV].astype(BF16)
    dq_copies, dq_receives = to_all(dq_rows.at[me], dq_rows, dq_send, dq_recv)
    for copy in dq_copies():
        copy.start()

    pick_lane = lax.broadcasted_iota(jnp.int32, (1, npick), 1)
    pick_pos = jnp.full((1, npick), -1, jnp.int32)
    for k in range(halo + 1):
        values = slot_pos(k)
        for r in range(POS_DEV):
            pick_pos = jnp.where(
                pick_lane == k * POS_DEV + r, (me - k) * tokens + values[r], pick_pos
            )
    seen = (pick_pos >= row_start[: 2 * tokens, :1]) & (pick_pos <= row_pos[: 2 * tokens, :1])
    for h in range(heads):
        cols = slice(h * HD, (h + 1) * HD)
        keys = kp[:, :, cols].reshape(npick, HD).astype(BF16)
        values = vp[:, :, cols].reshape(npick, HD).astype(BF16)
        query = qa[h, : 2 * tokens]
        grad = ga[h, : 2 * tokens]
        bent = jnp.tanh(dot_nt(query, keys) * (scale_q / soft_cap))
        prob = jnp.where(seen, jnp.exp(soft_cap * bent), 0.0) / zs[h, : 2 * tokens, :1]
        dscore = prob * (dot_nt(grad, values) - deltas[h][: 2 * tokens]) * (1.0 - bent * bent)
        dv = dot_tn(prob.astype(BF16), grad)
        dk = scale_q * dot_tn(dscore.astype(BF16), query)
        count = (halo + 1) * POS_DEV
        part[:, :, cols] = dk[:count].reshape(halo + 1, POS_DEV, HD)
        vcols = slice(kv_width + h * HD, kv_width + (h + 1) * HD)
        part[:, :, vcols] = dv[:count].reshape(halo + 1, POS_DEV, HD)

    def part_copy(k):
        return send(
            part.at[k], part_in.at[k - 1], pt_send.at[k - 1], pt_recv.at[k - 1],
            ctx=lax.rem(me - k + n, n),
        )

    for k in range(halo, 0, -1):
        part_copy(k).start()
    for load in loads:
        load.wait()
    for copy in dq_receives():
        copy.wait_recv()

    def all_rows(ref):
        return ref[...].astype(F32).reshape(positions, ref.shape[2]).astype(BF16)

    grad_part = dot_nt(all_rows(dq_rows), wq[...])
    grad_part = grad_part + jnp.where(core == 0, up_ref[...].astype(F32), 0.0)

    for copy in st_receives():
        copy.wait_recv()
    rank_state = st_all[0]
    for i in range(1, n):
        rank_state = rank_state + st_all[i]
    bias_row = lax.broadcasted_iota(jnp.int32, rank_state.shape, 0)
    for r in range(bias_ref.shape[0]):
        rank_state = rank_state + jnp.where(bias_row == r, bias_ref[r], 0.0)
    rank_state = rank_state[:, :positions]

    total = part[0]
    for k in range(1, halo + 1):
        part_copy(k).wait_recv()
        total = total + part_in[k - 1]
    kv_rows[me] = total.astype(BF16)
    kv_copies, kv_receives = to_all(kv_rows.at[me], kv_rows, kv_send, kv_recv)
    for copy in kv_copies():
        copy.start()
    for copy in kv_receives():
        copy.wait_recv()
    rows_kv = all_rows(kv_rows)
    grad_part = grad_part + dot_nt(rows_kv[:, :kv_width], wk[...])
    grad_part = grad_part + dot_nt(rows_kv[:, kv_width:], wv[...])

    my_slot = 2 * me + core
    if lanes > positions:
        rg_all[my_slot] = jnp.zeros(rg_all.shape[1:], F32)
    rg_all[my_slot, :, :positions] = dot_nt(rot_ref[...], grad_part, HIGHEST)

    def rank_copy(i, k, flip, receive):
        slot = my_slot
        other = jnp.where(flip == 1, 1 - core, core)
        if receive:
            slot = 2 * lax.rem(me - k + n, n) + other
        return send(
            rg_all.at[my_slot], rg_all.at[slot], rg_send.at[i], rg_recv.at[slot],
            ctx=lax.rem(me + k, n), head=other,
        )

    pairs = [(k, flip) for k in range(n) for flip in range(2) if k or flip]
    for i, (k, flip) in enumerate(pairs):
        rank_copy(i, k, flip, False).start()
    if gr_own.shape[1] > width:
        gr_own[...] = jnp.zeros(gr_own.shape, F32)
    gr_own[:, :width] = jnp.dot(
        rank_state, grad_part, precision=HIGHEST, preferred_element_type=F32
    )
    rot_copy = send(gr_own, gr_in, gr_send, gr_recv, head=1 - core)
    rot_copy.start()
    for i, (k, flip) in enumerate(pairs):
        rank_copy(i, k, flip, True).wait_recv()
    rank_grad = rg_all[0]
    for i in range(1, 2 * n):
        rank_grad = rank_grad + rg_all[i]
    rank_grad = rank_grad[:, :positions]
    grad_proj = jnp.dot(rank_grad, hidden_wide, precision=HIGHEST, preferred_element_type=F32)
    proj_out[...] = grad_proj
    bias_out[...] = jnp.sum(rank_grad, axis=1, keepdims=True)
    rot_copy.wait_recv()
    rot_out[...] = (gr_own[...] + gr_in[...])[:, :width] - grad_proj

    rot_copy.wait_send()
    for i, (k, flip) in enumerate(pairs):
        rank_copy(i, k, flip, False).wait_send()
    for copies in (st_copies, dq_copies, kv_copies):
        for copy in copies():
            copy.wait_send()
    for k in range(1, halo + 1):
        part_copy(k).wait_send()
    for j in range(1, chain + 1):
        for p in range(2):
            chain_copy(j, p).wait_send()
    for j in range(chain + 1):
        exchange(j, lambda copy: copy.wait_send())


def local(n, *args):
    queries, key_states = args[0], args[1]
    hidden, rotation = args[6], args[11]
    tokens, q_width = queries.shape
    kv_width = key_states.shape[1]
    heads = kv_width // HD
    width = hidden.shape[1]
    rank = rotation.shape[0]
    halo = n // 2
    chain = halo // 2
    positions = n * POS_DEV
    lanes = round_up(positions, LANES)
    wide = round_up(width, LANES)
    pick_slots = round_up((halo + 1) * POS_DEV, LANES) // POS_DEV
    rows = 2 * tokens + 2 * POS_DEV
    vmem = pl.BlockSpec(memory_space=pltpu.VMEM)
    smem = pl.BlockSpec(memory_space=pltpu.SMEM)
    hbm = pl.BlockSpec(memory_space=pl.ANY)
    dma = pltpu.SemaphoreType.DMA
    rot, proj, bias = pl.pallas_call(
        functools.partial(kernel, n),
        out_shape=(
            jax.ShapeDtypeStruct((rank, width), F32),
            jax.ShapeDtypeStruct((rank, width), F32),
            jax.ShapeDtypeStruct((rank, 1), F32),
        ),
        in_specs=[vmem] * 4 + [smem] * 2 + [vmem] * 2 + [hbm] * 3 + [vmem] * 2 + [smem],
        out_specs=(vmem, vmem, vmem),
        scratch_shapes=[
            pltpu.VMEM((halo + 1, tokens, kv_width), BF16),
            pltpu.VMEM((halo + 1, tokens, kv_width), BF16),
            pltpu.VMEM((heads, rows, HD), BF16),
            pltpu.VMEM((heads, rows, HD), BF16),
            pltpu.VMEM((heads, rows, HD), F32),
            pltpu.VMEM((heads, rows, LANES), F32),
            pltpu.VMEM((heads, 4 * POS_DEV, HD), F32),
            pltpu.VMEM((pick_slots, POS_DEV, kv_width), F32),
            pltpu.VMEM((pick_slots, POS_DEV, kv_width), F32),
            pltpu.VMEM((halo + 1, POS_DEV, 2 * kv_width), F32),
            pltpu.VMEM((halo, POS_DEV, 2 * kv_width), F32),
            pltpu.VMEM((n, POS_DEV, q_width), BF16),
            pltpu.VMEM((n, POS_DEV, 2 * kv_width), BF16),
            pltpu.VMEM((n, rank, lanes), F32),
            pltpu.VMEM((2 * n, rank, lanes), F32),
            pltpu.VMEM((rank, wide), F32),
            pltpu.VMEM((rank, wide), F32),
            pltpu.VMEM((width, q_width), BF16),
            pltpu.VMEM((width, kv_width), BF16),
            pltpu.VMEM((width, kv_width), BF16),
            dma((3,)),
            dma((chain, 2)), dma((chain, 2)),
            dma((chain, 2)), dma((chain, 2)),
            dma((n,)), dma((n,)),
            dma((n,)), dma((n,)),
            dma((halo,)), dma((halo,)),
            dma((n,)), dma((n,)),
            dma((2 * n,)), dma((2 * n,)),
            dma, dma,
        ],
        compiler_params=pltpu.CompilerParams(
            collective_id=0, has_side_effects=True, vmem_limit_bytes=52 << 20
        ),
        name="rank_backward",
    )(*args)
    return rot, proj, bias.reshape(rank)


def solution(mesh):
    in_specs = (
        P(("groups", "ctx"), "head"),
        P(("groups", "ctx"), "head"),
        P(("groups", "ctx"), "head"),
        P(("groups", "ctx"), "head"),
        P("groups"),
        P("groups"),
        P("groups", "ctx"),
        P("groups", "ctx"),
        P("ctx", "head"),
        P("ctx", "head"),
        P("ctx", "head"),
        P(None, "ctx"),
        P(None, "ctx"),
        P(),
    )
    out_specs = (P("groups", "ctx"), P("groups", "ctx"), P("groups"))
    return jax.shard_map(
        functools.partial(local, mesh.shape["ctx"]),
        mesh=mesh, in_specs=in_specs, out_specs=out_specs, check_vma=False,
    )
```

```python
import functools

import jax
import jax.numpy as jnp
from jax import lax
from jax.experimental import pallas as pl
from jax.experimental.pallas import tpu as pltpu
from jax.sharding import PartitionSpec as P

HD = 128
BLK = 64
POS_DEV = 8
LANES = 128

scale_q = 1.0 / 12.0
soft_cap = 50.0

MESH = pl.DeviceIdType.MESH
HIGHEST = lax.Precision.HIGHEST
F32 = jnp.float32
BF16 = jnp.bfloat16


def round_up(value, multiple):
    return (value + multiple - 1) // multiple * multiple


def dot_nt(left, right, precision=None):
    return lax.dot_general(
        left, right, (((1,), (1,)), ((), ())), preferred_element_type=F32, precision=precision
    )


def dot_tn(left, right):
    return lax.dot_general(left, right, (((0,), (0,)), ((), ())), preferred_element_type=F32)


def kernel(
    n,
    q_hbm, k_hbm, v_hbm, g_hbm, doc_hbm, pos_hbm, hidden_hbm, up_hbm,
    wq_hbm, wk_hbm, wv_hbm, rot_hbm, proj_hbm, bias_hbm,
    rot_out, proj_out, bias_out,
    kbuf, vbuf, qa, ga, num, zs, ms, kp, vp, part, part_in, dq_rows, kv_rows,
    st_all, rg_all, gr_own, gr_in, wq, wk, wv,
    q_ref, g_ref, doc_ref, pos_ref, hidden_ref, up_ref, rot_ref, proj_ref, bias_ref,
    w_sem, ch_send, ch_recv, ex_send, ex_recv, st_send, st_recv, dq_send, dq_recv,
    pt_send, pt_recv, kv_send, kv_recv, rg_send, rg_recv, gr_send, gr_recv,
):
    me = lax.axis_index("ctx")
    core = lax.axis_index("head")
    odd = lax.rem(me, 2)
    partner = me + 1 - 2 * odd
    after = lax.rem(me + 2, n)
    halo = n // 2
    chain = halo // 2
    tokens = q_ref.shape[0]
    kv_width = kbuf.shape[2]
    heads = kv_width // HD
    positions = n * POS_DEV
    lanes = st_all.shape[2]
    width = hidden_ref.shape[1]
    rows = 2 * tokens + 2 * POS_DEV
    npick = kp.shape[0] * POS_DEV

    barrier = pltpu.get_barrier_semaphore()
    for k in range(1, n):
        for c in range(2):
            pl.semaphore_signal(
                barrier, inc=1, device_id={"ctx": lax.rem(me + k, n), "head": c},
                device_id_type=MESH,
            )
    pl.semaphore_signal(barrier, inc=1, device_id={"head": 1 - core}, device_id_type=MESH)

    pairs_in = (
        (k_hbm, kbuf.at[0]), (v_hbm, vbuf.at[0]), (doc_hbm, doc_ref), (pos_hbm, pos_ref),
        (q_hbm, q_ref), (g_hbm, g_ref), (rot_hbm, rot_ref), (proj_hbm, proj_ref),
        (hidden_hbm, hidden_ref), (bias_hbm, bias_ref), (up_hbm, up_ref),
        (wq_hbm, wq), (wk_hbm, wk), (wv_hbm, wv),
    )
    loads = [
        pltpu.make_async_copy(src, dst, w_sem.at[i]) for i, (src, dst) in enumerate(pairs_in)
    ]
    for load in loads:
        load.start()

    def send(src, dst, send_sem, recv_sem, **where):
        return pltpu.make_async_remote_copy(
            src_ref=src, dst_ref=dst, send_sem=send_sem, recv_sem=recv_sem,
            device_id=where, device_id_type=MESH,
        )

    bufs = (kbuf, vbuf)

    def chain_copy(j, p):
        return send(
            bufs[p].at[2 * j - 2], bufs[p].at[2 * j], ch_send.at[j - 1, p],
            ch_recv.at[j - 1, p], ctx=after,
        )

    def exchange_copy(j, p, to_slot, m):
        return send(
            bufs[p].at[2 * j], bufs[p].at[to_slot], ex_send.at[m, p], ex_recv.at[m, p],
            ctx=partner,
        )

    def exchange(j, run):
        if j < chain:
            @pl.when(odd == 0)
            def _():
                for p in range(2):
                    run(exchange_copy(j, p, 2 * j + 1, j))
        if j > 0:
            @pl.when(odd == 1)
            def _():
                for p in range(2):
                    run(exchange_copy(j, p, 2 * j - 1, j - 1))

    loads[0].wait()
    loads[1].wait()
    pl.semaphore_wait(barrier, 2 * n - 1)

    for p in range(2):
        chain_copy(1, p).start()
    exchange(0, lambda copy: copy.start())

    row8 = lax.broadcasted_iota(jnp.int32, (POS_DEV, LANES), 0)
    lane8 = lax.broadcasted_iota(jnp.int32, (POS_DEV, LANES), 1)

    for load in loads[2:10]:
        load.wait()

    def slot_pos(k):
        block = lax.rem(me - k + n, n)
        return [pos_ref[block * POS_DEV + r] for r in range(POS_DEV)]

    def column(values):
        out = jnp.zeros((POS_DEV, LANES), jnp.int32)
        for r in range(POS_DEV):
            out = jnp.where(row8 == r, values[r], out)
        return out

    def one_hot(values):
        return jnp.where(column(values) == lane8, 1.0, 0.0).astype(BF16)

    blocks = tokens // BLK
    starts = []
    for b in range(blocks):
        mine = doc_ref[me * blocks + b]
        starts.append(
            lax.fori_loop(
                0, doc_ref.shape[0],
                lambda i, s, mine=mine: s + jnp.where(doc_ref[i] < mine, BLK, 0),
                jnp.int32(0),
            )
        )

    def start_of(position):
        out = jnp.zeros(position.shape, jnp.int32) + starts[0]
        for b in range(1, blocks):
            out = jnp.where(position >= b * BLK, starts[b], out)
        return out

    mine = column(slot_pos(0))
    own = lax.broadcasted_iota(jnp.int32, (tokens, LANES), 0)
    local_pos = jnp.concatenate([own, own, mine, mine], axis=0)
    row_pos = local_pos + me * tokens
    row_start = start_of(local_pos)
    lane_all = lax.broadcasted_iota(jnp.int32, (rows, LANES), 1)

    pick = one_hot(slot_pos(0))
    q_pick = jnp.dot(pick, q_ref[...], preferred_element_type=F32)
    g_pick = jnp.dot(pick, g_ref[...], preferred_element_type=F32)
    for h in range(heads):
        a, b, c = 2 * h * HD, (2 * h + 1) * HD, (2 * h + 2) * HD
        for dst, src, picked in ((qa, q_ref, q_pick), (ga, g_ref, g_pick)):
            dst[h, :tokens] = src[:, a:b]
            dst[h, tokens : 2 * tokens] = src[:, b:c]
            dst[h, 2 * tokens :] = jnp.concatenate(
                [picked[:, a:b], picked[:, b:c]], axis=0
            ).astype(BF16)

    hidden_wide = hidden_ref[...].astype(F32)
    state = dot_nt(proj_ref[...] - rot_ref[...], hidden_wide, HIGHEST)
    if lanes > positions:
        st_all[me] = jnp.zeros(st_all.shape[1:], F32)
    st_all[me, :, :positions] = state

    def to_all(src, dst, send_sems, recv_sems):
        def copies():
            return [
                send(
                    src, dst.at[me], send_sems.at[k - 1], recv_sems.at[me],
                    ctx=lax.rem(me + k, n),
                )
                for k in range(1, n)
            ]

        def receives():
            return [
                send(
                    src, dst.at[lax.rem(me - k + n, n)], send_sems.at[k - 1],
                    recv_sems.at[lax.rem(me - k + n, n)], ctx=lax.rem(me + k, n),
                )
                for k in range(1, n)
            ]

        return copies, receives

    st_copies, st_receives = to_all(st_all.at[me], st_all, st_send, st_recv)
    for copy in st_copies():
        copy.start()

    if npick > (halo + 1) * POS_DEV:
        kp[halo + 1 :] = jnp.zeros((kp.shape[0] - halo - 1,) + kp.shape[1:], F32)
        vp[halo + 1 :] = jnp.zeros((vp.shape[0] - halo - 1,) + vp.shape[1:], F32)

    def visit(k):
        base = (me - k) * tokens
        key_pos = lane_all + base
        visible = (key_pos >= row_start) & (key_pos <= row_pos)
        hot = one_hot(slot_pos(k))
        kp[k] = jnp.dot(hot, kbuf[k], preferred_element_type=F32)
        vp[k] = jnp.dot(hot, vbuf[k], preferred_element_type=F32)
        for h in range(heads):
            cols = slice(h * HD, (h + 1) * HD)
            keys = kbuf[k, :, cols]
            values = vbuf[k, :, cols]
            bent = jnp.tanh(dot_nt(qa[h], keys) * (scale_q / soft_cap))
            weights = jnp.where(visible, jnp.exp(soft_cap * bent), 0.0)
            num_new = jnp.dot(weights.astype(BF16), values, preferred_element_type=F32)
            bent_pick = bent[2 * tokens :]
            side = weights[2 * tokens :] * (1.0 - bent_pick * bent_pick)
            main = side * dot_nt(ga[h, 2 * tokens :], values)
            both = jnp.concatenate([main, side], axis=0).astype(BF16)
            ms_new = jnp.dot(both, keys, preferred_element_type=F32)
            if k == 0:
                zs[h], num[h], ms[h] = weights, num_new, ms_new
            else:
                zs[h] += weights
                num[h] += num_new
                ms[h] += ms_new

    visit(0)
    for j in range(1, chain + 1):
        for p in range(2):
            chain_copy(j, p).wait_recv()
            if j < chain:
                chain_copy(j + 1, p).start()
        exchange(j, lambda copy: copy.start())
        visit(2 * j)
        for p in range(2):
            send(
                bufs[p].at[0], bufs[p].at[2 * j - 1], ex_send.at[j - 1, p],
                ex_recv.at[j - 1, p], ctx=partner,
            ).wait_recv()
        visit(2 * j - 1)

    deltas = []
    for h in range(heads):
        total = jnp.sum(zs[h], axis=1, keepdims=True)
        zs[h] = jnp.broadcast_to(total, (rows, LANES))
        inv = num[h] / total
        delta = jnp.sum(ga[h].astype(F32) * inv, axis=1, keepdims=True)
        deltas.append(delta)
        d_pick = delta[2 * tokens :]
        main, side = ms[h, : 2 * POS_DEV], ms[h, 2 * POS_DEV :]
        dq = scale_q * (main - d_pick * side) / zs[h, 2 * tokens :]
        for i in range(2):
            at = (2 * h + i) * HD
            dq_rows[me, :, at : at + HD] = dq[i * POS_DEV : (i + 1) * POS_DEV].astype(BF16)
    dq_copies, dq_receives = to_all(dq_rows.at[me], dq_rows, dq_send, dq_recv)
    for copy in dq_copies():
        copy.start()

    pick_lane = lax.broadcasted_iota(jnp.int32, (1, npick), 1)
    pick_pos = jnp.full((1, npick), -1, jnp.int32)
    for k in range(halo + 1):
        values = slot_pos(k)
        for r in range(POS_DEV):
            pick_pos = jnp.where(
                pick_lane == k * POS_DEV + r, (me - k) * tokens + values[r], pick_pos
            )
    seen = (pick_pos >= row_start[: 2 * tokens, :1]) & (pick_pos <= row_pos[: 2 * tokens, :1])
    for h in range(heads):
        cols = slice(h * HD, (h + 1) * HD)
        keys = kp[:, :, cols].reshape(npick, HD).astype(BF16)
        values = vp[:, :, cols].reshape(npick, HD).astype(BF16)
        query = qa[h, : 2 * tokens]
        grad = ga[h, : 2 * tokens]
        bent = jnp.tanh(dot_nt(query, keys) * (scale_q / soft_cap))
        prob = jnp.where(seen, jnp.exp(soft_cap * bent), 0.0) / zs[h, : 2 * tokens, :1]
        dscore = prob * (dot_nt(grad, values) - deltas[h][: 2 * tokens]) * (1.0 - bent * bent)
        dv = dot_tn(prob.astype(BF16), grad)
        dk = scale_q * dot_tn(dscore.astype(BF16), query)
        count = (halo + 1) * POS_DEV
        part[:, :, cols] = dk[:count].reshape(halo + 1, POS_DEV, HD)
        vcols = slice(kv_width + h * HD, kv_width + (h + 1) * HD)
        part[:, :, vcols] = dv[:count].reshape(halo + 1, POS_DEV, HD)

    def part_copy(k):
        return send(
            part.at[k], part_in.at[k - 1], pt_send.at[k - 1], pt_recv.at[k - 1],
            ctx=lax.rem(me - k + n, n),
        )

    for k in range(halo, 0, -1):
        part_copy(k).start()
    for load in loads[10:]:
        load.wait()
    for copy in dq_receives():
        copy.wait_recv()

    def all_rows(ref):
        return ref[...].astype(F32).reshape(positions, ref.shape[2]).astype(BF16)

    grad_part = dot_nt(all_rows(dq_rows), wq[...])
    grad_part = grad_part + jnp.where(core == 0, up_ref[...].astype(F32), 0.0)

    for copy in st_receives():
        copy.wait_recv()
    rank_state = st_all[0]
    for i in range(1, n):
        rank_state = rank_state + st_all[i]
    bias_row = lax.broadcasted_iota(jnp.int32, rank_state.shape, 0)
    for r in range(bias_ref.shape[0]):
        rank_state = rank_state + jnp.where(bias_row == r, bias_ref[r], 0.0)
    rank_state = rank_state[:, :positions]

    total = part[0]
    for k in range(1, halo + 1):
        part_copy(k).wait_recv()
        total = total + part_in[k - 1]
    kv_rows[me] = total.astype(BF16)
    kv_copies, kv_receives = to_all(kv_rows.at[me], kv_rows, kv_send, kv_recv)
    for copy in kv_copies():
        copy.start()
    for copy in kv_receives():
        copy.wait_recv()
    rows_kv = all_rows(kv_rows)
    grad_part = grad_part + dot_nt(rows_kv[:, :kv_width], wk[...])
    grad_part = grad_part + dot_nt(rows_kv[:, kv_width:], wv[...])

    my_slot = 2 * me + core
    if lanes > positions:
        rg_all[my_slot] = jnp.zeros(rg_all.shape[1:], F32)
    rg_all[my_slot, :, :positions] = dot_nt(rot_ref[...], grad_part, HIGHEST)

    def rank_copy(i, k, flip, receive):
        slot = my_slot
        other = jnp.where(flip == 1, 1 - core, core)
        if receive:
            slot = 2 * lax.rem(me - k + n, n) + other
        return send(
            rg_all.at[my_slot], rg_all.at[slot], rg_send.at[i], rg_recv.at[slot],
            ctx=lax.rem(me + k, n), head=other,
        )

    pairs = [(k, flip) for k in range(n) for flip in range(2) if k or flip]
    for i, (k, flip) in enumerate(pairs):
        rank_copy(i, k, flip, False).start()
    if gr_own.shape[1] > width:
        gr_own[...] = jnp.zeros(gr_own.shape, F32)
    gr_own[:, :width] = jnp.dot(
        rank_state, grad_part, precision=HIGHEST, preferred_element_type=F32
    )
    rot_copy = send(gr_own, gr_in, gr_send, gr_recv, head=1 - core)
    rot_copy.start()
    for i, (k, flip) in enumerate(pairs):
        rank_copy(i, k, flip, True).wait_recv()
    rank_grad = rg_all[0]
    for i in range(1, 2 * n):
        rank_grad = rank_grad + rg_all[i]
    rank_grad = rank_grad[:, :positions]
    grad_proj = jnp.dot(rank_grad, hidden_wide, precision=HIGHEST, preferred_element_type=F32)
    proj_out[...] = grad_proj
    for r in range(bias_out.shape[0]):
        bias_out[r] = jnp.sum(rank_grad[r : r + 1])
    rot_copy.wait_recv()
    rot_out[...] = (gr_own[...] + gr_in[...])[:, :width] - grad_proj

    rot_copy.wait_send()
    for i, (k, flip) in enumerate(pairs):
        rank_copy(i, k, flip, False).wait_send()
    for copies in (st_copies, dq_copies, kv_copies):
        for copy in copies():
            copy.wait_send()
    for k in range(1, halo + 1):
        part_copy(k).wait_send()
    for j in range(1, chain + 1):
        for p in range(2):
            chain_copy(j, p).wait_send()
    for j in range(chain + 1):
        exchange(j, lambda copy: copy.wait_send())


def local(n, *args):
    queries, key_states = args[0], args[1]
    hidden, rotation = args[6], args[11]
    tokens, q_width = queries.shape
    kv_width = key_states.shape[1]
    heads = kv_width // HD
    width = hidden.shape[1]
    rank = rotation.shape[0]
    halo = n // 2
    chain = halo // 2
    positions = n * POS_DEV
    lanes = round_up(positions, LANES)
    wide = round_up(width, LANES)
    pick_slots = round_up((halo + 1) * POS_DEV, LANES) // POS_DEV
    rows = 2 * tokens + 2 * POS_DEV
    vmem = pl.BlockSpec(memory_space=pltpu.VMEM)
    smem = pl.BlockSpec(memory_space=pltpu.SMEM)
    hbm = pl.BlockSpec(memory_space=pltpu.HBM)
    dma = pltpu.SemaphoreType.DMA
    rot, proj, bias = pl.pallas_call(
        functools.partial(kernel, n),
        out_shape=(
            jax.ShapeDtypeStruct((rank, width), F32),
            jax.ShapeDtypeStruct((rank, width), F32),
            jax.ShapeDtypeStruct((rank,), F32),
        ),
        in_specs=[hbm] * len(args),
        out_specs=(vmem, vmem, smem),
        scratch_shapes=[
            pltpu.VMEM((halo + 1, tokens, kv_width), BF16),
            pltpu.VMEM((halo + 1, tokens, kv_width), BF16),
            pltpu.VMEM((heads, rows, HD), BF16),
            pltpu.VMEM((heads, rows, HD), BF16),
            pltpu.VMEM((heads, rows, HD), F32),
            pltpu.VMEM((heads, rows, LANES), F32),
            pltpu.VMEM((heads, 4 * POS_DEV, HD), F32),
            pltpu.VMEM((pick_slots, POS_DEV, kv_width), F32),
            pltpu.VMEM((pick_slots, POS_DEV, kv_width), F32),
            pltpu.VMEM((halo + 1, POS_DEV, 2 * kv_width), F32),
            pltpu.VMEM((halo, POS_DEV, 2 * kv_width), F32),
            pltpu.VMEM((n, POS_DEV, q_width), BF16),
            pltpu.VMEM((n, POS_DEV, 2 * kv_width), BF16),
            pltpu.VMEM((n, rank, lanes), F32),
            pltpu.VMEM((2 * n, rank, lanes), F32),
            pltpu.VMEM((rank, wide), F32),
            pltpu.VMEM((rank, wide), F32),
            pltpu.VMEM((width, q_width), BF16),
            pltpu.VMEM((width, kv_width), BF16),
            pltpu.VMEM((width, kv_width), BF16),
            pltpu.VMEM((tokens, q_width), BF16),
            pltpu.VMEM((tokens, q_width), BF16),
            pltpu.SMEM(args[4].shape, jnp.int32),
            pltpu.SMEM(args[5].shape, jnp.int32),
            pltpu.VMEM(hidden.shape, BF16),
            pltpu.VMEM(hidden.shape, BF16),
            pltpu.VMEM(rotation.shape, F32),
            pltpu.VMEM(rotation.shape, F32),
            pltpu.SMEM((rank,), F32),
            dma((len(args),)),
            dma((chain, 2)), dma((chain, 2)),
            dma((chain, 2)), dma((chain, 2)),
            dma((n,)), dma((n,)),
            dma((n,)), dma((n,)),
            dma((halo,)), dma((halo,)),
            dma((n,)), dma((n,)),
            dma((2 * n,)), dma((2 * n,)),
            dma, dma,
        ],
        compiler_params=pltpu.CompilerParams(
            collective_id=0, has_side_effects=True, vmem_limit_bytes=64 << 20
        ),
        name="rank_backward",
    )(*args)
    return rot, proj, bias


def solution(mesh):
    in_specs = (
        P(("groups", "ctx"), "head"),
        P(("groups", "ctx"), "head"),
        P(("groups", "ctx"), "head"),
        P(("groups", "ctx"), "head"),
        P("groups"),
        P("groups"),
        P("groups", "ctx"),
        P("groups", "ctx"),
        P("ctx", "head"),
        P("ctx", "head"),
        P("ctx", "head"),
        P(None, "ctx"),
        P(None, "ctx"),
        P(),
    )
    out_specs = (P("groups", "ctx"), P("groups", "ctx"), P("groups"))
    return jax.shard_map(
        functools.partial(local, mesh.shape["ctx"]),
        mesh=mesh, in_specs=in_specs, out_specs=out_specs, check_vma=False,
    )
```

```python
import functools

import jax
import jax.numpy as jnp
from jax import lax
from jax.experimental import pallas as pl
from jax.experimental.pallas import tpu as pltpu
from jax.sharding import PartitionSpec as P

HD = 128
BLK = 64
POS_DEV = 8
LANES = 128
PIECES = 4

scale_q = 1.0 / 12.0
soft_cap = 50.0

MESH = pl.DeviceIdType.MESH
HIGHEST = lax.Precision.HIGHEST
F32 = jnp.float32
BF16 = jnp.bfloat16


def round_up(value, multiple):
    return (value + multiple - 1) // multiple * multiple


def dot_nt(left, right, precision=None):
    return lax.dot_general(
        left, right, (((1,), (1,)), ((), ())), preferred_element_type=F32, precision=precision
    )


def dot_tn(left, right):
    return lax.dot_general(left, right, (((0,), (0,)), ((), ())), preferred_element_type=F32)


def kernel(
    n,
    q_hbm, k_hbm, v_hbm, g_hbm, doc_hbm, pos_hbm, hidden_hbm, up_hbm,
    wq_hbm, wk_hbm, wv_hbm, rot_hbm, proj_hbm, bias_hbm,
    rot_out, proj_out, bias_out,
    kbuf, vbuf, qa, ga, num, zs, ms, kp, vp, part, part_in, dq_rows, kv_rows,
    st_all, rg_all, gr_own, gr_in, wq, wk, wv,
    q_ref, g_ref, doc_ref, pos_ref, hidden_ref, up_ref, rot_ref, proj_ref, bias_ref,
    w_sem, ch_send, ch_recv, ex_send, ex_recv, st_send, st_recv, dq_send, dq_recv,
    pt_send, pt_recv, kv_send, kv_recv, rg_send, rg_recv, gr_send, gr_recv,
):
    me = lax.axis_index("ctx")
    core = lax.axis_index("head")
    odd = lax.rem(me, 2)
    partner = me + 1 - 2 * odd
    after = lax.rem(me + 2, n)
    halo = n // 2
    chain = halo // 2
    tokens = q_ref.shape[0]
    kv_width = kbuf.shape[2]
    heads = kv_width // HD
    positions = n * POS_DEV
    lanes = st_all.shape[2]
    width = hidden_ref.shape[1]
    rows = 2 * tokens + 2 * POS_DEV
    npick = kp.shape[0] * POS_DEV

    barrier = pltpu.get_barrier_semaphore()
    for k in range(1, n):
        for c in range(2):
            pl.semaphore_signal(
                barrier, inc=1, device_id={"ctx": lax.rem(me + k, n), "head": c},
                device_id_type=MESH,
            )
    pl.semaphore_signal(barrier, inc=1, device_id={"head": 1 - core}, device_id_type=MESH)

    pairs_in = (
        (k_hbm, kbuf.at[0]), (v_hbm, vbuf.at[0]), (doc_hbm, doc_ref), (pos_hbm, pos_ref),
        (q_hbm, q_ref), (g_hbm, g_ref), (rot_hbm, rot_ref), (proj_hbm, proj_ref),
        (hidden_hbm, hidden_ref), (bias_hbm, bias_ref), (up_hbm, up_ref),
        (wq_hbm, wq), (wk_hbm, wk), (wv_hbm, wv),
    )
    loads = [
        pltpu.make_async_copy(src, dst, w_sem.at[i]) for i, (src, dst) in enumerate(pairs_in)
    ]
    for load in loads:
        load.start()

    def send(src, dst, send_sem, recv_sem, **where):
        return pltpu.make_async_remote_copy(
            src_ref=src, dst_ref=dst, send_sem=send_sem, recv_sem=recv_sem,
            device_id=where, device_id_type=MESH,
        )

    half = tokens // 2

    def piece(p, slot):
        return (kbuf, vbuf)[p // 2].at[slot, pl.ds(p % 2 * half, half)]

    def chain_copy(j, p):
        return send(
            piece(p, 2 * j - 2), piece(p, 2 * j), ch_send.at[j - 1, p],
            ch_recv.at[j - 1, p], ctx=after,
        )

    def exchange_copy(j, p, to_slot, m):
        return send(
            piece(p, 2 * j), piece(p, to_slot), ex_send.at[m, p], ex_recv.at[m, p],
            ctx=partner,
        )

    def exchange(j, p, run):
        if j < chain:
            @pl.when(odd == 0)
            def _():
                run(exchange_copy(j, p, 2 * j + 1, j))
        if j > 0:
            @pl.when(odd == 1)
            def _():
                run(exchange_copy(j, p, 2 * j - 1, j - 1))

    loads[0].wait()
    loads[1].wait()
    pl.semaphore_wait(barrier, 2 * n - 1)

    for p in range(PIECES):
        chain_copy(1, p).start()
        exchange(0, p, lambda copy: copy.start())

    row8 = lax.broadcasted_iota(jnp.int32, (POS_DEV, LANES), 0)
    lane8 = lax.broadcasted_iota(jnp.int32, (POS_DEV, LANES), 1)

    for load in loads[2:10]:
        load.wait()

    def slot_pos(k):
        block = lax.rem(me - k + n, n)
        return [pos_ref[block * POS_DEV + r] for r in range(POS_DEV)]

    def column(values):
        out = jnp.zeros((POS_DEV, LANES), jnp.int32)
        for r in range(POS_DEV):
            out = jnp.where(row8 == r, values[r], out)
        return out

    def one_hot(values):
        return jnp.where(column(values) == lane8, 1.0, 0.0).astype(BF16)

    blocks = tokens // BLK
    starts = []
    for b in range(blocks):
        mine = doc_ref[me * blocks + b]
        starts.append(
            lax.fori_loop(
                0, doc_ref.shape[0],
                lambda i, s, mine=mine: s + jnp.where(doc_ref[i] < mine, BLK, 0),
                jnp.int32(0),
            )
        )

    def start_of(position):
        out = jnp.zeros(position.shape, jnp.int32) + starts[0]
        for b in range(1, blocks):
            out = jnp.where(position >= b * BLK, starts[b], out)
        return out

    mine = column(slot_pos(0))
    own = lax.broadcasted_iota(jnp.int32, (tokens, LANES), 0)
    local_pos = jnp.concatenate([own, own, mine, mine], axis=0)
    row_pos = local_pos + me * tokens
    row_start = start_of(local_pos)
    lane_all = lax.broadcasted_iota(jnp.int32, (rows, LANES), 1)

    pick = one_hot(slot_pos(0))
    q_pick = jnp.dot(pick, q_ref[...], preferred_element_type=F32)
    g_pick = jnp.dot(pick, g_ref[...], preferred_element_type=F32)
    for h in range(heads):
        a, b, c = 2 * h * HD, (2 * h + 1) * HD, (2 * h + 2) * HD
        for dst, src, picked in ((qa, q_ref, q_pick), (ga, g_ref, g_pick)):
            dst[h, :tokens] = src[:, a:b]
            dst[h, tokens : 2 * tokens] = src[:, b:c]
            dst[h, 2 * tokens :] = jnp.concatenate(
                [picked[:, a:b], picked[:, b:c]], axis=0
            ).astype(BF16)

    hidden_wide = hidden_ref[...].astype(F32)
    state = dot_nt(proj_ref[...] - rot_ref[...], hidden_wide, HIGHEST)
    if lanes > positions:
        st_all[me] = jnp.zeros(st_all.shape[1:], F32)
    st_all[me, :, :positions] = state

    def to_all(src, dst, send_sems, recv_sems):
        def copies():
            return [
                send(
                    src, dst.at[me], send_sems.at[k - 1], recv_sems.at[me],
                    ctx=lax.rem(me + k, n),
                )
                for k in range(1, n)
            ]

        def receives():
            return [
                send(
                    src, dst.at[lax.rem(me - k + n, n)], send_sems.at[k - 1],
                    recv_sems.at[lax.rem(me - k + n, n)], ctx=lax.rem(me + k, n),
                )
                for k in range(1, n)
            ]

        return copies, receives

    st_copies, st_receives = to_all(st_all.at[me], st_all, st_send, st_recv)
    for copy in st_copies():
        copy.start()

    if npick > (halo + 1) * POS_DEV:
        kp[halo + 1 :] = jnp.zeros((kp.shape[0] - halo - 1,) + kp.shape[1:], F32)
        vp[halo + 1 :] = jnp.zeros((vp.shape[0] - halo - 1,) + vp.shape[1:], F32)

    def visit(k):
        base = (me - k) * tokens
        key_pos = lane_all + base
        visible = (key_pos >= row_start) & (key_pos <= row_pos)
        hot = one_hot(slot_pos(k))
        kp[k] = jnp.dot(hot, kbuf[k], preferred_element_type=F32)
        vp[k] = jnp.dot(hot, vbuf[k], preferred_element_type=F32)
        for h in range(heads):
            cols = slice(h * HD, (h + 1) * HD)
            keys = kbuf[k, :, cols]
            values = vbuf[k, :, cols]
            bent = jnp.tanh(dot_nt(qa[h], keys) * (scale_q / soft_cap))
            weights = jnp.where(visible, jnp.exp(soft_cap * bent), 0.0)
            num_new = jnp.dot(weights.astype(BF16), values, preferred_element_type=F32)
            bent_pick = bent[2 * tokens :]
            side = weights[2 * tokens :] * (1.0 - bent_pick * bent_pick)
            main = side * dot_nt(ga[h, 2 * tokens :], values)
            both = jnp.concatenate([main, side], axis=0).astype(BF16)
            ms_new = jnp.dot(both, keys, preferred_element_type=F32)
            if k == 0:
                zs[h], num[h], ms[h] = weights, num_new, ms_new
            else:
                zs[h] += weights
                num[h] += num_new
                ms[h] += ms_new

    visit(0)
    for j in range(1, chain + 1):
        for p in range(PIECES):
            chain_copy(j, p).wait_recv()
            if j < chain:
                chain_copy(j + 1, p).start()
            exchange(j, p, lambda copy: copy.start())
        visit(2 * j)
        if j == 1:
            for copy in st_receives():
                copy.wait_recv()
            rank_state = st_all[0]
            for i in range(1, n):
                rank_state = rank_state + st_all[i]
            bias_row = lax.broadcasted_iota(jnp.int32, rank_state.shape, 0)
            for r in range(bias_ref.shape[0]):
                rank_state = rank_state + jnp.where(bias_row == r, bias_ref[r], 0.0)
            rank_state = rank_state[:, :positions]
            loads[10].wait()
            up = jnp.where(core == 0, up_ref[...].astype(F32), 0.0)
            rank_up = dot_nt(rot_ref[...], up, HIGHEST)
            rot_up = jnp.dot(rank_state, up, precision=HIGHEST, preferred_element_type=F32)
        for p in range(PIECES):
            send(
                piece(p, 0), piece(p, 2 * j - 1), ex_send.at[j - 1, p],
                ex_recv.at[j - 1, p], ctx=partner,
            ).wait_recv()
        visit(2 * j - 1)

    deltas = []
    for h in range(heads):
        total = jnp.sum(zs[h], axis=1, keepdims=True)
        zs[h] = jnp.broadcast_to(total, (rows, LANES))
        inv = num[h] / total
        delta = jnp.sum(ga[h].astype(F32) * inv, axis=1, keepdims=True)
        deltas.append(delta)
        d_pick = delta[2 * tokens :]
        main, side = ms[h, : 2 * POS_DEV], ms[h, 2 * POS_DEV :]
        dq = scale_q * (main - d_pick * side) / zs[h, 2 * tokens :]
        for i in range(2):
            at = (2 * h + i) * HD
            dq_rows[me, :, at : at + HD] = dq[i * POS_DEV : (i + 1) * POS_DEV].astype(BF16)
    dq_copies, dq_receives = to_all(dq_rows.at[me], dq_rows, dq_send, dq_recv)
    for copy in dq_copies():
        copy.start()

    pick_lane = lax.broadcasted_iota(jnp.int32, (1, npick), 1)
    pick_pos = jnp.full((1, npick), -1, jnp.int32)
    for k in range(halo + 1):
        values = slot_pos(k)
        for r in range(POS_DEV):
            pick_pos = jnp.where(
                pick_lane == k * POS_DEV + r, (me - k) * tokens + values[r], pick_pos
            )
    seen = (pick_pos >= row_start[: 2 * tokens, :1]) & (pick_pos <= row_pos[: 2 * tokens, :1])
    for h in range(heads):
        cols = slice(h * HD, (h + 1) * HD)
        keys = kp[:, :, cols].reshape(npick, HD).astype(BF16)
        values = vp[:, :, cols].reshape(npick, HD).astype(BF16)
        query = qa[h, : 2 * tokens]
        grad = ga[h, : 2 * tokens]
        bent = jnp.tanh(dot_nt(query, keys) * (scale_q / soft_cap))
        prob = jnp.where(seen, jnp.exp(soft_cap * bent), 0.0) / zs[h, : 2 * tokens, :1]
        dscore = prob * (dot_nt(grad, values) - deltas[h][: 2 * tokens]) * (1.0 - bent * bent)
        dv = dot_tn(prob.astype(BF16), grad)
        dk = scale_q * dot_tn(dscore.astype(BF16), query)
        count = (halo + 1) * POS_DEV
        part[:, :, cols] = dk[:count].reshape(halo + 1, POS_DEV, HD)
        vcols = slice(kv_width + h * HD, kv_width + (h + 1) * HD)
        part[:, :, vcols] = dv[:count].reshape(halo + 1, POS_DEV, HD)

    def part_copy(k):
        return send(
            part.at[k], part_in.at[k - 1], pt_send.at[k - 1], pt_recv.at[k - 1],
            ctx=lax.rem(me - k + n, n),
        )

    for k in range(halo, 0, -1):
        part_copy(k).start()
    for load in loads[11:]:
        load.wait()
    for copy in dq_receives():
        copy.wait_recv()

    def all_rows(ref):
        return ref[...].astype(F32).reshape(positions, ref.shape[2]).astype(BF16)

    grad_part = dot_nt(wq[...], all_rows(dq_rows))

    total = part[0]
    for k in range(1, halo + 1):
        part_copy(k).wait_recv()
        total = total + part_in[k - 1]
    kv_rows[me] = total.astype(BF16)
    kv_copies, kv_receives = to_all(kv_rows.at[me], kv_rows, kv_send, kv_recv)
    for copy in kv_copies():
        copy.start()
    for copy in kv_receives():
        copy.wait_recv()
    rows_kv = all_rows(kv_rows)
    grad_part = grad_part + dot_nt(wk[...], rows_kv[:, :kv_width])
    grad_part = grad_part + dot_nt(wv[...], rows_kv[:, kv_width:])

    my_slot = 2 * me + core
    if lanes > positions:
        rg_all[my_slot] = jnp.zeros(rg_all.shape[1:], F32)
    rg_all[my_slot, :, :positions] = rank_up + jnp.dot(
        rot_ref[...], grad_part, precision=HIGHEST, preferred_element_type=F32
    )

    def rank_copy(i, k, flip, receive):
        slot = my_slot
        other = jnp.where(flip == 1, 1 - core, core)
        if receive:
            slot = 2 * lax.rem(me - k + n, n) + other
        return send(
            rg_all.at[my_slot], rg_all.at[slot], rg_send.at[i], rg_recv.at[slot],
            ctx=lax.rem(me + k, n), head=other,
        )

    pairs = [(k, flip) for k in range(n) for flip in range(2) if k or flip]
    for i, (k, flip) in enumerate(pairs):
        rank_copy(i, k, flip, False).start()
    if gr_own.shape[1] > width:
        gr_own[...] = jnp.zeros(gr_own.shape, F32)
    gr_own[:, :width] = rot_up + dot_nt(rank_state, grad_part, HIGHEST)
    rot_copy = send(gr_own, gr_in, gr_send, gr_recv, head=1 - core)
    rot_copy.start()
    for i, (k, flip) in enumerate(pairs):
        rank_copy(i, k, flip, True).wait_recv()
    rank_grad = rg_all[0]
    for i in range(1, 2 * n):
        rank_grad = rank_grad + rg_all[i]
    rank_grad = rank_grad[:, :positions]
    grad_proj = jnp.dot(rank_grad, hidden_wide, precision=HIGHEST, preferred_element_type=F32)
    proj_out[...] = grad_proj
    for r in range(bias_out.shape[0]):
        bias_out[r] = jnp.sum(rank_grad[r : r + 1])
    rot_copy.wait_recv()
    rot_out[...] = (gr_own[...] + gr_in[...])[:, :width] - grad_proj

    rot_copy.wait_send()
    for i, (k, flip) in enumerate(pairs):
        rank_copy(i, k, flip, False).wait_send()
    for copies in (st_copies, dq_copies, kv_copies):
        for copy in copies():
            copy.wait_send()
    for k in range(1, halo + 1):
        part_copy(k).wait_send()
    for j in range(1, chain + 1):
        for p in range(PIECES):
            chain_copy(j, p).wait_send()
    for j in range(chain + 1):
        for p in range(PIECES):
            exchange(j, p, lambda copy: copy.wait_send())


def finish(rot_in, proj_in, bias_in, rot_out, proj_out, bias_out, sems):
    copies = [
        pltpu.make_async_copy(src, dst, sems.at[i])
        for i, (src, dst) in enumerate(
            ((rot_in, rot_out), (proj_in, proj_out), (bias_in, bias_out))
        )
    ]
    for copy in copies:
        copy.start()
    for copy in copies:
        copy.wait()


def local(n, *args):
    queries, key_states = args[0], args[1]
    hidden, rotation = args[6], args[11]
    tokens, q_width = queries.shape
    kv_width = key_states.shape[1]
    heads = kv_width // HD
    width = hidden.shape[1]
    rank = rotation.shape[0]
    halo = n // 2
    chain = halo // 2
    positions = n * POS_DEV
    lanes = round_up(positions, LANES)
    wide = round_up(width, LANES)
    pick_slots = round_up((halo + 1) * POS_DEV, LANES) // POS_DEV
    rows = 2 * tokens + 2 * POS_DEV
    vmem = pl.BlockSpec(memory_space=pltpu.VMEM)
    smem = pl.BlockSpec(memory_space=pltpu.SMEM)
    hbm = pl.BlockSpec(memory_space=pltpu.HBM)
    dma = pltpu.SemaphoreType.DMA
    outs = pl.pallas_call(
        functools.partial(kernel, n),
        out_shape=(
            jax.ShapeDtypeStruct((rank, width), F32),
            jax.ShapeDtypeStruct((rank, width), F32),
            jax.ShapeDtypeStruct((rank,), F32),
        ),
        in_specs=[hbm] * len(args),
        out_specs=(vmem, vmem, smem),
        scratch_shapes=[
            pltpu.VMEM((halo + 1, tokens, kv_width), BF16),
            pltpu.VMEM((halo + 1, tokens, kv_width), BF16),
            pltpu.VMEM((heads, rows, HD), BF16),
            pltpu.VMEM((heads, rows, HD), BF16),
            pltpu.VMEM((heads, rows, HD), F32),
            pltpu.VMEM((heads, rows, LANES), F32),
            pltpu.VMEM((heads, 4 * POS_DEV, HD), F32),
            pltpu.VMEM((pick_slots, POS_DEV, kv_width), F32),
            pltpu.VMEM((pick_slots, POS_DEV, kv_width), F32),
            pltpu.VMEM((halo + 1, POS_DEV, 2 * kv_width), F32),
            pltpu.VMEM((halo, POS_DEV, 2 * kv_width), F32),
            pltpu.VMEM((n, POS_DEV, q_width), BF16),
            pltpu.VMEM((n, POS_DEV, 2 * kv_width), BF16),
            pltpu.VMEM((n, rank, lanes), F32),
            pltpu.VMEM((2 * n, rank, lanes), F32),
            pltpu.VMEM((rank, wide), F32),
            pltpu.VMEM((rank, wide), F32),
            pltpu.VMEM((width, q_width), BF16),
            pltpu.VMEM((width, kv_width), BF16),
            pltpu.VMEM((width, kv_width), BF16),
            pltpu.VMEM((tokens, q_width), BF16),
            pltpu.VMEM((tokens, q_width), BF16),
            pltpu.SMEM(args[4].shape, jnp.int32),
            pltpu.SMEM(args[5].shape, jnp.int32),
            pltpu.VMEM(hidden.shape, BF16),
            pltpu.VMEM(hidden.shape, BF16),
            pltpu.VMEM(rotation.shape, F32),
            pltpu.VMEM(rotation.shape, F32),
            pltpu.SMEM((rank,), F32),
            dma((len(args),)),
            dma((chain, PIECES)), dma((chain, PIECES)),
            dma((chain, PIECES)), dma((chain, PIECES)),
            dma((n,)), dma((n,)),
            dma((n,)), dma((n,)),
            dma((halo,)), dma((halo,)),
            dma((n,)), dma((n,)),
            dma((2 * n,)), dma((2 * n,)),
            dma, dma,
        ],
        compiler_params=pltpu.CompilerParams(
            collective_id=0, has_side_effects=True, vmem_limit_bytes=64 << 20
        ),
        name="rank_backward",
    )(*args)
    return pl.pallas_call(
        finish,
        out_shape=tuple(jax.ShapeDtypeStruct(out.shape, out.dtype) for out in outs),
        in_specs=[hbm] * 3,
        out_specs=(hbm,) * 3,
        scratch_shapes=[dma((3,))],
        name="finish",
    )(*outs)


def solution(mesh):
    in_specs = (
        P(("groups", "ctx"), "head"),
        P(("groups", "ctx"), "head"),
        P(("groups", "ctx"), "head"),
        P(("groups", "ctx"), "head"),
        P("groups"),
        P("groups"),
        P("groups", "ctx"),
        P("groups", "ctx"),
        P("ctx", "head"),
        P("ctx", "head"),
        P("ctx", "head"),
        P(None, "ctx"),
        P(None, "ctx"),
        P(),
    )
    out_specs = (P("groups", "ctx"), P("groups", "ctx"), P("groups"))
    return jax.shard_map(
        functools.partial(local, mesh.shape["ctx"]),
        mesh=mesh, in_specs=in_specs, out_specs=out_specs, check_vma=False,
    )
```

```python
import functools

import jax
import jax.numpy as jnp
from jax import lax
from jax.experimental import pallas as pl
from jax.experimental.pallas import tpu as pltpu
from jax.sharding import PartitionSpec as P

HD = 128
BLK = 64
POS_DEV = 8
LANES = 128
PIECES = 4

scale_q = 1.0 / 12.0
soft_cap = 50.0

MESH = pl.DeviceIdType.MESH
HIGHEST = lax.Precision.HIGHEST
F32 = jnp.float32
BF16 = jnp.bfloat16


def round_up(value, multiple):
    return (value + multiple - 1) // multiple * multiple


def dot_nt(left, right, precision=None):
    return lax.dot_general(
        left, right, (((1,), (1,)), ((), ())), preferred_element_type=F32, precision=precision
    )


def dot_tn(left, right):
    return lax.dot_general(left, right, (((0,), (0,)), ((), ())), preferred_element_type=F32)


def kernel(
    n,
    q_hbm, k_hbm, v_hbm, g_hbm, doc_hbm, pos_hbm, hidden_hbm, up_hbm,
    wq_hbm, wk_hbm, wv_hbm, rot_hbm, proj_hbm, bias_hbm,
    rot_out, proj_out, bias_out,
    kbuf, vbuf, qa, ga, num, zs, ms, kp, vp, part, part_in, dq_rows, kv_rows,
    st_all, rg_all, gr_own, gr_in, wq, wk, wv,
    q_ref, g_ref, doc_ref, pos_ref, hidden_ref, up_ref, rot_ref, proj_ref, bias_ref,
    w_sem, ch_send, ch_recv, ex_send, ex_recv, st_send, st_recv, dq_send, dq_recv,
    pt_send, pt_recv, kv_send, kv_recv, rg_send, rg_recv, gr_send, gr_recv,
):
    me = lax.axis_index("ctx")
    core = lax.axis_index("head")
    odd = lax.rem(me, 2)
    partner = me + 1 - 2 * odd
    after = lax.rem(me + 2, n)
    halo = n // 2
    chain = halo // 2
    tokens = q_ref.shape[0]
    kv_width = kbuf.shape[2]
    heads = kv_width // HD
    positions = n * POS_DEV
    lanes = st_all.shape[2]
    width = hidden_ref.shape[1]
    rows = 2 * tokens + 2 * POS_DEV
    npick = kp.shape[0] * POS_DEV

    barrier = pltpu.get_barrier_semaphore()
    for k in range(1, n):
        for c in range(2):
            pl.semaphore_signal(
                barrier, inc=1, device_id={"ctx": lax.rem(me + k, n), "head": c},
                device_id_type=MESH,
            )
    pl.semaphore_signal(barrier, inc=1, device_id={"head": 1 - core}, device_id_type=MESH)

    pairs_in = (
        (k_hbm, kbuf.at[0]), (v_hbm, vbuf.at[0]), (doc_hbm, doc_ref), (pos_hbm, pos_ref),
        (q_hbm, q_ref), (g_hbm, g_ref), (rot_hbm, rot_ref), (proj_hbm, proj_ref),
        (hidden_hbm, hidden_ref), (bias_hbm, bias_ref), (up_hbm, up_ref),
        (wq_hbm, wq), (wk_hbm, wk), (wv_hbm, wv),
    )
    loads = [
        pltpu.make_async_copy(src, dst, w_sem.at[i]) for i, (src, dst) in enumerate(pairs_in)
    ]
    for load in loads:
        load.start()

    def send(src, dst, send_sem, recv_sem, **where):
        return pltpu.make_async_remote_copy(
            src_ref=src, dst_ref=dst, send_sem=send_sem, recv_sem=recv_sem,
            device_id=where, device_id_type=MESH,
        )

    half = tokens // 2

    def piece(p, slot):
        return (kbuf, vbuf)[p // 2].at[slot, pl.ds(p % 2 * half, half)]

    def chain_copy(j, p):
        return send(
            piece(p, 2 * j - 2), piece(p, 2 * j), ch_send.at[j - 1, p],
            ch_recv.at[j - 1, p], ctx=after,
        )

    def exchange_copy(j, p, to_slot, m):
        return send(
            piece(p, 2 * j), piece(p, to_slot), ex_send.at[m, p], ex_recv.at[m, p],
            ctx=partner,
        )

    def exchange(j, p, run):
        if j < chain:
            @pl.when(odd == 0)
            def _():
                run(exchange_copy(j, p, 2 * j + 1, j))
        if j > 0:
            @pl.when(odd == 1)
            def _():
                run(exchange_copy(j, p, 2 * j - 1, j - 1))

    loads[0].wait()
    loads[1].wait()
    pl.semaphore_wait(barrier, 2 * n - 1)

    for p in range(PIECES):
        chain_copy(1, p).start()
        exchange(0, p, lambda copy: copy.start())

    row8 = lax.broadcasted_iota(jnp.int32, (POS_DEV, LANES), 0)
    lane8 = lax.broadcasted_iota(jnp.int32, (POS_DEV, LANES), 1)

    for load in loads[2:10]:
        load.wait()

    def slot_pos(k):
        block = lax.rem(me - k + n, n)
        return [pos_ref[block * POS_DEV + r] for r in range(POS_DEV)]

    def column(values):
        out = jnp.zeros((POS_DEV, LANES), jnp.int32)
        for r in range(POS_DEV):
            out = jnp.where(row8 == r, values[r], out)
        return out

    def one_hot(values):
        return jnp.where(column(values) == lane8, 1.0, 0.0).astype(BF16)

    blocks = tokens // BLK
    starts = []
    for b in range(blocks):
        mine = doc_ref[me * blocks + b]
        starts.append(
            lax.fori_loop(
                0, doc_ref.shape[0],
                lambda i, s, mine=mine: s + jnp.where(doc_ref[i] < mine, BLK, 0),
                jnp.int32(0),
            )
        )

    def start_of(position):
        out = jnp.zeros(position.shape, jnp.int32) + starts[0]
        for b in range(1, blocks):
            out = jnp.where(position >= b * BLK, starts[b], out)
        return out

    mine = column(slot_pos(0))
    own = lax.broadcasted_iota(jnp.int32, (tokens, LANES), 0)
    local_pos = jnp.concatenate([own, own, mine, mine], axis=0)
    row_pos = local_pos + me * tokens
    row_start = start_of(local_pos)
    lane_all = lax.broadcasted_iota(jnp.int32, (rows, LANES), 1)

    pick = one_hot(slot_pos(0))
    q_pick = jnp.dot(pick, q_ref[...], preferred_element_type=F32)
    g_pick = jnp.dot(pick, g_ref[...], preferred_element_type=F32)
    for h in range(heads):
        a, b, c = 2 * h * HD, (2 * h + 1) * HD, (2 * h + 2) * HD
        for dst, src, picked in ((qa, q_ref, q_pick), (ga, g_ref, g_pick)):
            dst[h, :tokens] = src[:, a:b]
            dst[h, tokens : 2 * tokens] = src[:, b:c]
            dst[h, 2 * tokens :] = jnp.concatenate(
                [picked[:, a:b], picked[:, b:c]], axis=0
            ).astype(BF16)

    hidden_wide = hidden_ref[...].astype(F32)
    state = dot_nt(proj_ref[...] - rot_ref[...], hidden_wide, HIGHEST)
    if lanes > positions:
        st_all[me] = jnp.zeros(st_all.shape[1:], F32)
    st_all[me, :, :positions] = state

    def to_all(src, dst, send_sems, recv_sems):
        def copies():
            return [
                send(
                    src, dst.at[me], send_sems.at[k - 1], recv_sems.at[me],
                    ctx=lax.rem(me + k, n),
                )
                for k in range(1, n)
            ]

        def receives():
            return [
                send(
                    src, dst.at[lax.rem(me - k + n, n)], send_sems.at[k - 1],
                    recv_sems.at[lax.rem(me - k + n, n)], ctx=lax.rem(me + k, n),
                )
                for k in range(1, n)
            ]

        return copies, receives

    st_copies, st_receives = to_all(st_all.at[me], st_all, st_send, st_recv)
    for copy in st_copies():
        copy.start()

    if npick > (halo + 1) * POS_DEV:
        kp[halo + 1 :] = jnp.zeros((kp.shape[0] - halo - 1,) + kp.shape[1:], F32)
        vp[halo + 1 :] = jnp.zeros((vp.shape[0] - halo - 1,) + vp.shape[1:], F32)

    def visit(k):
        base = (me - k) * tokens
        key_pos = lane_all + base
        visible = (key_pos >= row_start) & (key_pos <= row_pos)
        hot = one_hot(slot_pos(k))
        kp[k] = jnp.dot(hot, kbuf[k], preferred_element_type=F32)
        vp[k] = jnp.dot(hot, vbuf[k], preferred_element_type=F32)
        for h in range(heads):
            cols = slice(h * HD, (h + 1) * HD)
            keys = kbuf[k, :, cols]
            values = vbuf[k, :, cols]
            bent = jnp.tanh(dot_nt(qa[h], keys) * (scale_q / soft_cap))
            weights = jnp.where(visible, jnp.exp(soft_cap * bent), 0.0)
            num_new = jnp.dot(weights.astype(BF16), values, preferred_element_type=F32)
            bent_pick = bent[2 * tokens :]
            side = weights[2 * tokens :] * (1.0 - bent_pick * bent_pick)
            main = side * dot_nt(ga[h, 2 * tokens :], values)
            both = jnp.concatenate([main, side], axis=0).astype(BF16)
            ms_new = jnp.dot(both, keys, preferred_element_type=F32)
            if k == 0:
                zs[h], num[h], ms[h] = weights, num_new, ms_new
            else:
                zs[h] += weights
                num[h] += num_new
                ms[h] += ms_new

    visit(0)
    for j in range(1, chain + 1):
        for p in range(PIECES):
            chain_copy(j, p).wait_recv()
            if j < chain:
                chain_copy(j + 1, p).start()
            exchange(j, p, lambda copy: copy.start())
        visit(2 * j)
        if j == 1:
            for copy in st_receives():
                copy.wait_recv()
            rank_state = st_all[0]
            for i in range(1, n):
                rank_state = rank_state + st_all[i]
            bias_row = lax.broadcasted_iota(jnp.int32, rank_state.shape, 0)
            for r in range(bias_ref.shape[0]):
                rank_state = rank_state + jnp.where(bias_row == r, bias_ref[r], 0.0)
            rank_state = rank_state[:, :positions]
            loads[10].wait()
            up = jnp.where(core == 0, up_ref[...].astype(F32), 0.0)
            rank_up = dot_nt(rot_ref[...], up, HIGHEST)
            rot_up = jnp.dot(rank_state, up, precision=HIGHEST, preferred_element_type=F32)
        for p in range(PIECES):
            send(
                piece(p, 0), piece(p, 2 * j - 1), ex_send.at[j - 1, p],
                ex_recv.at[j - 1, p], ctx=partner,
            ).wait_recv()
        visit(2 * j - 1)

    deltas = []
    for h in range(heads):
        total = jnp.sum(zs[h], axis=1, keepdims=True)
        zs[h] = jnp.broadcast_to(total, (rows, LANES))
        inv = num[h] / total
        delta = jnp.sum(ga[h].astype(F32) * inv, axis=1, keepdims=True)
        deltas.append(delta)
        d_pick = delta[2 * tokens :]
        main, side = ms[h, : 2 * POS_DEV], ms[h, 2 * POS_DEV :]
        dq = scale_q * (main - d_pick * side) / zs[h, 2 * tokens :]
        for i in range(2):
            at = (2 * h + i) * HD
            dq_rows[me, :, at : at + HD] = dq[i * POS_DEV : (i + 1) * POS_DEV].astype(BF16)
    dq_copies, dq_receives = to_all(dq_rows.at[me], dq_rows, dq_send, dq_recv)
    for copy in dq_copies():
        copy.start()

    pick_lane = lax.broadcasted_iota(jnp.int32, (1, npick), 1)
    pick_pos = jnp.full((1, npick), -1, jnp.int32)
    for k in range(halo + 1):
        values = slot_pos(k)
        for r in range(POS_DEV):
            pick_pos = jnp.where(
                pick_lane == k * POS_DEV + r, (me - k) * tokens + values[r], pick_pos
            )
    seen = (pick_pos >= row_start[: 2 * tokens, :1]) & (pick_pos <= row_pos[: 2 * tokens, :1])
    for h in range(heads):
        cols = slice(h * HD, (h + 1) * HD)
        keys = kp[:, :, cols].reshape(npick, HD).astype(BF16)
        values = vp[:, :, cols].reshape(npick, HD).astype(BF16)
        query = qa[h, : 2 * tokens]
        grad = ga[h, : 2 * tokens]
        bent = jnp.tanh(dot_nt(query, keys) * (scale_q / soft_cap))
        prob = jnp.where(seen, jnp.exp(soft_cap * bent), 0.0) / zs[h, : 2 * tokens, :1]
        dscore = prob * (dot_nt(grad, values) - deltas[h][: 2 * tokens]) * (1.0 - bent * bent)
        dv = dot_tn(prob.astype(BF16), grad)
        dk = scale_q * dot_tn(dscore.astype(BF16), query)
        count = (halo + 1) * POS_DEV
        part[:, :, cols] = dk[:count].reshape(halo + 1, POS_DEV, HD)
        vcols = slice(kv_width + h * HD, kv_width + (h + 1) * HD)
        part[:, :, vcols] = dv[:count].reshape(halo + 1, POS_DEV, HD)

    def part_copy(k):
        return send(
            part.at[k], part_in.at[k - 1], pt_send.at[k - 1], pt_recv.at[k - 1],
            ctx=lax.rem(me - k + n, n),
        )

    for k in range(halo, 0, -1):
        part_copy(k).start()
    for load in loads[11:]:
        load.wait()
    for copy in dq_receives():
        copy.wait_recv()

    def all_rows(ref):
        return ref[...].astype(F32).reshape(positions, ref.shape[2]).astype(BF16)

    grad_part = dot_nt(wq[...], all_rows(dq_rows))

    total = part[0]
    for k in range(1, halo + 1):
        part_copy(k).wait_recv()
        total = total + part_in[k - 1]
    kv_rows[me] = total.astype(BF16)
    kv_copies, kv_receives = to_all(kv_rows.at[me], kv_rows, kv_send, kv_recv)
    for copy in kv_copies():
        copy.start()
    for copy in kv_receives():
        copy.wait_recv()
    rows_kv = all_rows(kv_rows)
    grad_part = grad_part + dot_nt(wk[...], rows_kv[:, :kv_width])
    grad_part = grad_part + dot_nt(wv[...], rows_kv[:, kv_width:])

    my_slot = 2 * me + core
    if lanes > positions:
        rg_all[my_slot] = jnp.zeros(rg_all.shape[1:], F32)
    rg_all[my_slot, :, :positions] = rank_up + jnp.dot(
        rot_ref[...], grad_part, precision=HIGHEST, preferred_element_type=F32
    )

    def rank_copy(i, k, flip, receive):
        slot = my_slot
        other = jnp.where(flip == 1, 1 - core, core)
        if receive:
            slot = 2 * lax.rem(me - k + n, n) + other
        return send(
            rg_all.at[my_slot], rg_all.at[slot], rg_send.at[i], rg_recv.at[slot],
            ctx=lax.rem(me + k, n), head=other,
        )

    pairs = [(k, flip) for k in range(n) for flip in range(2) if k or flip]
    for i, (k, flip) in enumerate(pairs):
        rank_copy(i, k, flip, False).start()
    if gr_own.shape[1] > width:
        gr_own[...] = jnp.zeros(gr_own.shape, F32)
    gr_own[:, :width] = rot_up + dot_nt(rank_state, grad_part, HIGHEST)
    rot_copy = send(gr_own, gr_in, gr_send, gr_recv, head=1 - core)
    rot_copy.start()
    for i, (k, flip) in enumerate(pairs):
        rank_copy(i, k, flip, True).wait_recv()
    rank_grad = rg_all[0]
    for i in range(1, 2 * n):
        rank_grad = rank_grad + rg_all[i]
    rank_grad = rank_grad[:, :positions]
    grad_proj = jnp.dot(rank_grad, hidden_wide, precision=HIGHEST, preferred_element_type=F32)
    proj_out[...] = grad_proj
    for r in range(bias_out.shape[0]):
        bias_out[r] = jnp.sum(rank_grad[r : r + 1])
    rot_copy.wait_recv()
    rot_out[...] = (gr_own[...] + gr_in[...])[:, :width] - grad_proj

    rot_copy.wait_send()
    for i, (k, flip) in enumerate(pairs):
        rank_copy(i, k, flip, False).wait_send()
    for copies in (st_copies, dq_copies, kv_copies):
        for copy in copies():
            copy.wait_send()
    for k in range(1, halo + 1):
        part_copy(k).wait_send()
    for j in range(1, chain + 1):
        for p in range(PIECES):
            chain_copy(j, p).wait_send()
    for j in range(chain + 1):
        for p in range(PIECES):
            exchange(j, p, lambda copy: copy.wait_send())


def finish(rot_in, proj_in, bias_in, rot_out, proj_out, bias_out):
    rot_out[...] = rot_in[...]
    proj_out[...] = proj_in[...]
    bias_out[...] = bias_in[...]


def local(n, *args):
    queries, key_states = args[0], args[1]
    hidden, rotation = args[6], args[11]
    tokens, q_width = queries.shape
    kv_width = key_states.shape[1]
    heads = kv_width // HD
    width = hidden.shape[1]
    rank = rotation.shape[0]
    halo = n // 2
    chain = halo // 2
    positions = n * POS_DEV
    lanes = round_up(positions, LANES)
    wide = round_up(width, LANES)
    pick_slots = round_up((halo + 1) * POS_DEV, LANES) // POS_DEV
    rows = 2 * tokens + 2 * POS_DEV
    vmem = pl.BlockSpec(memory_space=pltpu.VMEM)
    smem = pl.BlockSpec(memory_space=pltpu.SMEM)
    hbm = pl.BlockSpec(memory_space=pltpu.HBM)
    dma = pltpu.SemaphoreType.DMA
    outs = pl.pallas_call(
        functools.partial(kernel, n),
        out_shape=(
            jax.ShapeDtypeStruct((rank, width), F32),
            jax.ShapeDtypeStruct((rank, width), F32),
            jax.ShapeDtypeStruct((rank,), F32),
        ),
        in_specs=[hbm] * len(args),
        out_specs=(vmem, vmem, smem),
        scratch_shapes=[
            pltpu.VMEM((halo + 1, tokens, kv_width), BF16),
            pltpu.VMEM((halo + 1, tokens, kv_width), BF16),
            pltpu.VMEM((heads, rows, HD), BF16),
            pltpu.VMEM((heads, rows, HD), BF16),
            pltpu.VMEM((heads, rows, HD), F32),
            pltpu.VMEM((heads, rows, LANES), F32),
            pltpu.VMEM((heads, 4 * POS_DEV, HD), F32),
            pltpu.VMEM((pick_slots, POS_DEV, kv_width), F32),
            pltpu.VMEM((pick_slots, POS_DEV, kv_width), F32),
            pltpu.VMEM((halo + 1, POS_DEV, 2 * kv_width), F32),
            pltpu.VMEM((halo, POS_DEV, 2 * kv_width), F32),
            pltpu.VMEM((n, POS_DEV, q_width), BF16),
            pltpu.VMEM((n, POS_DEV, 2 * kv_width), BF16),
            pltpu.VMEM((n, rank, lanes), F32),
            pltpu.VMEM((2 * n, rank, lanes), F32),
            pltpu.VMEM((rank, wide), F32),
            pltpu.VMEM((rank, wide), F32),
            pltpu.VMEM((width, q_width), BF16),
            pltpu.VMEM((width, kv_width), BF16),
            pltpu.VMEM((width, kv_width), BF16),
            pltpu.VMEM((tokens, q_width), BF16),
            pltpu.VMEM((tokens, q_width), BF16),
            pltpu.SMEM(args[4].shape, jnp.int32),
            pltpu.SMEM(args[5].shape, jnp.int32),
            pltpu.VMEM(hidden.shape, BF16),
            pltpu.VMEM(hidden.shape, BF16),
            pltpu.VMEM(rotation.shape, F32),
            pltpu.VMEM(rotation.shape, F32),
            pltpu.SMEM((rank,), F32),
            dma((len(args),)),
            dma((chain, PIECES)), dma((chain, PIECES)),
            dma((chain, PIECES)), dma((chain, PIECES)),
            dma((n,)), dma((n,)),
            dma((n,)), dma((n,)),
            dma((halo,)), dma((halo,)),
            dma((n,)), dma((n,)),
            dma((2 * n,)), dma((2 * n,)),
            dma, dma,
        ],
        compiler_params=pltpu.CompilerParams(
            collective_id=0, has_side_effects=True, vmem_limit_bytes=64 << 20
        ),
        name="rank_backward",
    )(*args)
    return pl.pallas_call(
        finish,
        out_shape=tuple(jax.ShapeDtypeStruct(out.shape, out.dtype) for out in outs),
        in_specs=[vmem] * 3,
        out_specs=(vmem,) * 3,
        name="finish",
    )(*outs)


def solution(mesh):
    in_specs = (
        P(("groups", "ctx"), "head"),
        P(("groups", "ctx"), "head"),
        P(("groups", "ctx"), "head"),
        P(("groups", "ctx"), "head"),
        P("groups"),
        P("groups"),
        P("groups", "ctx"),
        P("groups", "ctx"),
        P("ctx", "head"),
        P("ctx", "head"),
        P("ctx", "head"),
        P(None, "ctx"),
        P(None, "ctx"),
        P(),
    )
    out_specs = (P("groups", "ctx"), P("groups", "ctx"), P("groups"))
    return jax.shard_map(
        functools.partial(local, mesh.shape["ctx"]),
        mesh=mesh, in_specs=in_specs, out_specs=out_specs, check_vma=False,
    )
```
